32 devices in a mesh: row: 8 (over z, core), col: 4 (over y, x).
Axes of the slice: x: 2, y: 2, z: 4, core: 2. Of those that a mesh axis runs over, the one named last changes fastest.
Arguments:
- mode_basis: bfloat16 [4096, 4096], P('row'), may hold values from -0.125 to 0.125
- node_coords: float32 [3, 4096], P(None, 'row'), may hold values from -1 to 1
- quad_weights: float32 [4096], P('row'), may hold values from 0.3 to 3
- magnetization: bfloat16 [2, 4096, 32], P(None, 'col', 'row'), may hold values from -6 to 6
- decay_rates: float32 [4096], replicated, may hold values from 0.02 to 1.5
- directions: float32 [6, 3, 32], replicated, may hold values from -3 to 3
Outputs:
- final_magnet: bfloat16 [2, 4096, 32], P(None, 'col', 'row')
The draws below stay inside these ranges and needn't reach their ends.
All inputs are finite; a program needn't handle non-finite values.
Results may differ from the reference program's by a relative error of at most 0.03.
Values may be sent and summed in bfloat16 or wider, within the bound.
A program may use at most 64 MiB of HBM per device.

```python
import math
import jax
import jax.numpy as jnp
from jax import lax

MODES = 4096
STEPS = 3
NODES = 4096
WAVEFORMS = 32
N_ROW = 8


def strengthened(drawn, own_key, source, target, blocks, factor):
    owner, partner = [(jnp.arange(drawn.shape[position]) // (drawn.shape[position] // blocks)).reshape([-1 if axis == position else 1 for axis in range(drawn.ndim)]) for position in (source, target)]
    chosen = jax.random.permutation(own_key, blocks)[partner]
    strong = (owner == chosen) | (owner == (partner + blocks // 2) % blocks)
    return jnp.where(strong, factor * drawn, drawn)


def shard_levels(rng, dims, cuts, low, largest):
    gain, own = 1.0, jax.random.fold_in(rng, 6)
    for position, parts in cuts:
        heights = jnp.exp(jax.random.uniform(jax.random.fold_in(own, position), (parts,), jnp.float32, low / len(cuts), largest / len(cuts)))
        gain = gain * jnp.repeat(heights, dims[position] // parts).reshape([-1 if axis == position else 1 for axis in range(len(dims))])
    return gain


def normal_values(key, extent, scale, bound, cuts=(), kind=jnp.bfloat16):
    entries = jax.random.normal(key, extent, jnp.float32) * scale
    if len(cuts) > 0:
        entries = shard_levels(key, extent, cuts, -0.22, 0.18) * entries
    return jnp.clip(entries, min=-bound, max=bound).astype(kind)


def bell_draw_with(own_key, shape, spread, limit, cuts, heavy, kind=jnp.bfloat16):
    array = spread * jax.random.normal(own_key, shape, jnp.float32)
    if cuts:
        array = array * shard_levels(own_key, shape, cuts, -0.22, 0.18)
    return jnp.clip(strengthened(array, jax.random.fold_in(own_key, 3), *heavy), -limit, limit).astype(kind)


def setup_inputs(seed: int = 0) -> dict:
    arg_keys = jax.random.split(jax.random.key(seed), 7)
    return {
        "mode_basis": bell_draw_with(arg_keys[0], (NODES, MODES), NODES ** -0.5, 0.125, ((0, 8),), (0, 1, 8, 2.0)),
        "node_coords": jnp.clip(jax.random.uniform(arg_keys[1], (3, NODES), jnp.float32, -1.0, 1.0) * shard_levels(arg_keys[1], (3, NODES), ((1, 8),), -0.4, 0.0), -1.0, 1.0),
        "quad_weights": jnp.clip(jnp.exp(math.log(3.0) - 2.3025851 * jax.random.uniform(arg_keys[2], (NODES,), jnp.float32) ** shard_levels(arg_keys[2], (NODES,), ((0, 8),), -0.2, 0.2)), 0.3, 3.0),
        "magnetization": normal_values(arg_keys[3], (2, MODES, WAVEFORMS), 1.0, 6.0, ((1, 4), (2, 8))),
        "decay_rates": jnp.clip(jnp.exp(jax.random.uniform(arg_keys[4], (MODES,), jnp.float32, math.log(0.02), math.log(1.5))), 0.02, 1.5),
        "directions": normal_values(arg_keys[5], (2 * STEPS, 3, WAVEFORMS), 0.5, 3.0, (), jnp.float32),
    }


def reference(mode_basis, node_coords, quad_weights, magnetization, decay_rates, directions):
    moments = node_coords * quad_weights[None, :]
    slab_rows = NODES // N_ROW

    def add_slab(accum, slab_index):
        first_node = slab_index * slab_rows
        basis_slab = lax.dynamic_slice_in_dim(mode_basis, first_node, slab_rows, 0)
        moment_slab = lax.dynamic_slice_in_dim(moments, first_node, slab_rows, 1)
        pieces = []
        for axis_index in range(3):
            weighted = (basis_slab.astype(jnp.float32) * moment_slab[axis_index][:, None]).astype(jnp.bfloat16)
            partial_gram = lax.dot_general(basis_slab, weighted, (((0,), (0,)), ((), ())), preferred_element_type=jnp.float32)
            rounded = lax.optimization_barrier(partial_gram.astype(jnp.bfloat16))
            pieces.append(rounded.astype(jnp.float32))
        return accum + jnp.stack(pieces), None

    total_gram, _ = lax.scan(add_slab, jnp.zeros((3, MODES, MODES), jnp.float32), jnp.arange(N_ROW, dtype=jnp.int32))
    moment_gram = total_gram.astype(jnp.bfloat16)

    def apply_operator(field_now, weights_now, factor, keep_part):
        joined = jnp.concatenate([field_now[0], field_now[1]], axis=1)
        combined = jnp.zeros((MODES, 2 * WAVEFORMS), jnp.float32)
        for axis_index in range(3):
            scale_row = jnp.concatenate([weights_now[axis_index], weights_now[axis_index]])
            combined = combined + scale_row[None, :] * jnp.dot(moment_gram[axis_index], joined, preferred_element_type=jnp.float32)
        real_q = combined[:, :WAVEFORMS]
        imag_q = combined[:, WAVEFORMS:]
        diag_scale = (keep_part - factor * decay_rates)[:, None]
        field_float = field_now.astype(jnp.float32)
        new_real = factor * imag_q + diag_scale * field_float[0]
        new_imag = -factor * real_q + diag_scale * field_float[1]
        return jnp.stack([new_real, new_imag])

    field_now = magnetization
    for step_index in range(STEPS):
        half_field = apply_operator(field_now, directions[2 * step_index], 0.5, 1.0).astype(jnp.bfloat16)
        update = apply_operator(half_field, directions[2 * step_index + 1], 1.0, 0.0)
        field_now = (field_now.astype(jnp.float32) + update).astype(jnp.bfloat16)
    return field_now
```

```python
import functools

import jax
import jax.numpy as jnp
from jax import lax
from jax.experimental import pallas as pl
from jax.experimental.pallas import tpu as pltpu
from jax.sharding import PartitionSpec as P

STEPS = 3
MESH = pl.DeviceIdType.MESH
NT = (((1,), (1,)), ((), ()))
NN = (((1,), (0,)), ((), ()))


def kernel(
    R, C, basis_hbm, coords, quad, start, rates, dirs, out,
    basis, landed, joined, modes, parts, sums, weights, scaled, field, lastout, lastin,
    basis_sem, first_send, first_recv, sum_send, sum_recv, mode_send, mode_recv,
    last_send, last_recv,
):
    H = R // C
    r = lax.axis_index("row")
    c = lax.axis_index("col")
    wl = start.shape[1]
    rows = H * 2 * wl
    own = modes.shape[2]
    halves = 2 * STEPS

    basis_copy = pltpu.make_async_copy(basis_hbm, basis, basis_sem)
    basis_copy.start()

    barrier = pltpu.get_barrier_semaphore()
    home = r // H
    for d in range(1, R):
        pl.semaphore_signal(barrier, inc=1, device_id=(lax.rem(r + d, R), c), device_id_type=MESH)
    is_self = home == c

    def greet(row, col):
        @pl.when(jnp.logical_not((row == r) & (col == c)))
        def _():
            pl.semaphore_signal(barrier, inc=1, device_id=(row, col), device_id_type=MESH)

    for t in range(R):
        greet(jnp.int32(t), home)
    for h in range(H):
        for q in range(C):
            greet(H * c + h, jnp.int32(q))
    pl.semaphore_wait(barrier, 3 * R - 1 - 2 * is_self.astype(jnp.int32))

    slot = lax.rem(r, H) * C + c

    def first_copy(t):
        return pltpu.make_async_remote_copy(
            src_ref=start, dst_ref=landed.at[slot], send_sem=first_send.at[t],
            recv_sem=first_recv.at[slot], device_id=(jnp.int32(t), home), device_id_type=MESH,
        )

    def not_self(t):
        return jnp.logical_not((r == t) & is_self)

    for t in range(R):
        @pl.when(not_self(t))
        def _():
            first_copy(t).start()

    @pl.when(is_self)
    def _():
        pltpu.make_async_copy(start, landed.at[slot], first_recv.at[slot]).start()

    row_id = lax.broadcasted_iota(jnp.int32, (rows, dirs.shape[2]), 0)
    wave_id = lax.broadcasted_iota(jnp.int32, (rows, dirs.shape[2]), 1)
    wave = c * (H * wl) + (row_id // (2 * wl)) * wl + row_id % wl
    chosen = wave_id == wave
    for a in range(halves):
        column = [
            jnp.sum(jnp.where(chosen, dirs[a, k : k + 1, :], 0.0), axis=1, keepdims=True)
            for k in range(3)
        ]
        for i in range(quad.shape[0]):
            lanes = pl.ds(i * 128, 128)
            q = quad[i : i + 1, :]
            weights[a, :, lanes] = (
                column[0] * (coords[0:1, lanes] * q)
                + column[1] * (coords[1:2, lanes] * q)
                + column[2] * (coords[2:3, lanes] * q)
            )

    width = start.shape[2]
    for h in range(H):
        for q in range(C):
            pltpu.make_async_copy(start, landed.at[h * C + q], first_recv.at[h * C + q]).wait()
            for x in range(2):
                joined[pl.ds((h * 2 + x) * wl, wl), pl.ds(q * width, width)] = landed[
                    h * C + q, x
                ].astype(jnp.float32)
    basis_copy.wait()

    near = sorted(range(R), key=lambda d: min(d, R - d))

    def block(t):
        return pl.ds(pl.multiple_of(t * own, own), own)

    part_id = (lax.broadcasted_iota(jnp.int32, (rows, coords.shape[1]), 0) // wl) % 2

    def scale(total, a):
        v = total * weights[a]
        turned = jnp.where(part_id == 0, pltpu.roll(v, rows - wl, 0), -pltpu.roll(v, wl, 0))
        scaled[...] = turned.astype(jnp.bfloat16)

    total = jnp.zeros((rows, coords.shape[1]), jnp.float32)
    for d in near:
        t = lax.rem(r - d + R, R)
        piece = joined[:, block(t)]
        if d == 0:
            field[...] = piece
        piece = piece.astype(jnp.bfloat16)
        if d == 0:
            modes[0] = piece
        total = total + lax.dot_general(
            piece, basis[:, block(t)], NT, preferred_element_type=jnp.float32
        )
    scale(total, 0)

    def sum_copy(d):
        return pltpu.make_async_remote_copy(
            src_ref=parts.at[d], dst_ref=sums.at[d], send_sem=sum_send.at[d],
            recv_sem=sum_recv.at[d], device_id=(lax.rem(r + d, R), c), device_id_type=MESH,
        )

    def mode_copy(d):
        return pltpu.make_async_remote_copy(
            src_ref=modes.at[0], dst_ref=modes.at[d], send_sem=mode_send.at[d],
            recv_sem=mode_recv.at[d], device_id=(lax.rem(r + d, R), c), device_id_type=MESH,
        )

    def own_block(factor, keep):
        v = scaled[...]
        for d in reversed(near[1:]):
            t = lax.rem(r + d, R)
            parts[d] = lax.dot_general(
                v, basis[:, block(t)], NN, preferred_element_type=jnp.float32
            ).astype(jnp.bfloat16)
            sum_copy(d).start()
        acc = lax.dot_general(v, basis[:, block(r)], NN, preferred_element_type=jnp.float32)
        for d in near[1:]:
            sum_copy(d).wait_recv()
            acc = acc + sums[d].astype(jnp.float32)
        for d in near[1:]:
            sum_copy(d).wait_send()
        lam = jnp.concatenate(
            [rates[pl.ds(r * (own // 128) + i, 1), :] for i in range(own // 128)], axis=1
        )
        return factor * acc + (keep - factor * lam) * modes[0].astype(jnp.float32)

    def half_step(i, carry):
        odd = lax.rem(i, 2) == 1
        factor = jnp.where(odd, 1.0, 0.5).astype(jnp.float32)
        keep = jnp.where(odd, 0.0, 1.0).astype(jnp.float32)
        fresh = own_block(factor, keep)
        fresh = fresh + (1.0 - keep) * field[...]
        rounded = fresh.astype(jnp.bfloat16)
        modes[0] = rounded
        for d in reversed(near[1:]):
            mode_copy(d).start()

        @pl.when(odd)
        def _():
            field[...] = rounded.astype(jnp.float32)

        total = lax.dot_general(
            rounded, basis[:, block(r)], NT, preferred_element_type=jnp.float32
        )
        for d in near[1:]:
            mode_copy(d).wait_recv()
            total = total + lax.dot_general(
                modes[d], basis[:, block(lax.rem(r - d + R, R))], NT,
                preferred_element_type=jnp.float32,
            )
        scale(total, i + 1)
        for d in near[1:]:
            mode_copy(d).wait_send()
        return carry

    lax.fori_loop(0, halves - 1, half_step, 0)

    fresh = own_block(1.0, 0.0) + field[...]
    target_col = r // H
    q = lax.rem(r, H)

    def last_copy(h):
        return pltpu.make_async_remote_copy(
            src_ref=lastout.at[h], dst_ref=lastin.at[q], send_sem=last_send.at[h],
            recv_sem=last_recv.at[q], device_id=(H * c + h, target_col), device_id_type=MESH,
        )

    for h in range(H):
        for x in range(2):
            first = (h * 2 + x) * wl
            lastout[h, x] = fresh[first : first + wl, :].astype(jnp.bfloat16)
        local = (H * c + h == r) & (target_col == c)

        @pl.when(jnp.logical_not(local))
        def _():
            last_copy(h).start()

        @pl.when(local)
        def _():
            pltpu.make_async_copy(lastout.at[h], lastin.at[q], last_recv.at[q]).start()

    for s in range(H):
        pltpu.make_async_copy(lastout.at[0], lastin.at[s], last_recv.at[s]).wait()
        out[:, :, pl.ds(s * own, own)] = lastin[s]
    for h in range(H):
        @pl.when(jnp.logical_not((H * c + h == r) & (target_col == c)))
        def _():
            last_copy(h).wait_send()
    for t in range(R):
        @pl.when(not_self(t))
        def _():
            first_copy(t).wait_send()


def on_device(R, C, basis, coords, quad, magnetization, rates, dirs):
    H = R // C
    nodes, mode_count = basis.shape
    start = jnp.transpose(magnetization, (0, 2, 1))
    _, wl, width = start.shape
    rows = H * 2 * wl
    own = mode_count // R
    vmem = pl.BlockSpec(memory_space=pltpu.VMEM)
    dma = pltpu.SemaphoreType.DMA
    bf16, f32 = jnp.bfloat16, jnp.float32
    result = pl.pallas_call(
        functools.partial(kernel, R, C),
        out_shape=jax.ShapeDtypeStruct(start.shape, bf16),
        in_specs=[pl.BlockSpec(memory_space=pl.ANY)] + [vmem] * 5,
        out_specs=vmem,
        scratch_shapes=[
            pltpu.VMEM((nodes, mode_count), bf16),
            pltpu.VMEM((H * C, 2, wl, width), bf16),
            pltpu.VMEM((rows, mode_count), f32),
            pltpu.VMEM((R, rows, own), bf16),
            pltpu.VMEM((R, rows, own), bf16),
            pltpu.VMEM((R, rows, own), bf16),
            pltpu.VMEM((2 * STEPS, rows, nodes), f32),
            pltpu.VMEM((rows, nodes), bf16),
            pltpu.VMEM((rows, own), f32),
            pltpu.VMEM((H, 2, wl, own), bf16),
            pltpu.VMEM((H, 2, wl, own), bf16),
            dma,
            dma((R,)), dma((H * C,)),
            dma((R,)), dma((R,)), dma((R,)), dma((R,)),
            dma((H,)), dma((H,)),
        ],
        compiler_params=pltpu.CompilerParams(collective_id=0, has_side_effects=True),
    )(basis, coords, quad.reshape(-1, 128), start, rates.reshape(-1, 128), dirs)
    return jnp.transpose(result, (0, 2, 1))


def solution(mesh):
    return jax.shard_map(
        functools.partial(on_device, mesh.shape["row"], mesh.shape["col"]),
        mesh=mesh,
        in_specs=(P("row", None), P(None, "row"), P("row"), P(None, "col", "row"), P(), P()),
        out_specs=P(None, "col", "row"),
        check_vma=False,
    )
```

```python
import functools

import jax
import jax.numpy as jnp
from jax import lax
from jax.experimental import pallas as pl
from jax.experimental.pallas import tpu as pltpu
from jax.sharding import PartitionSpec as P

STEPS = 3
MESH = pl.DeviceIdType.MESH
NT = (((1,), (1,)), ((), ()))
NN = (((1,), (0,)), ((), ()))


def kernel(
    R, C, basis_hbm, coords, quad, start, rates, dirs, out,
    basis, landed, joined, modes, parts, sums, weights, scaled, field, acc, lastout, lastin,
    basis_sem, first_send, first_recv, sum_send, sum_recv, mode_send, mode_recv,
    last_send, last_recv,
):
    H = R // C
    r = lax.axis_index("row")
    c = lax.axis_index("col")
    wl = start.shape[1]
    rows = H * 2 * wl
    own = modes.shape[2]
    halves = 2 * STEPS

    basis_copy = pltpu.make_async_copy(basis_hbm, basis, basis_sem)
    basis_copy.start()

    barrier = pltpu.get_barrier_semaphore()
    home = r // H
    for d in range(1, R):
        pl.semaphore_signal(barrier, inc=1, device_id=(lax.rem(r + d, R), c), device_id_type=MESH)
    is_self = home == c

    def greet(row, col):
        @pl.when(jnp.logical_not((row == r) & (col == c)))
        def _():
            pl.semaphore_signal(barrier, inc=1, device_id=(row, col), device_id_type=MESH)

    for t in range(R):
        greet(jnp.int32(t), home)
    for h in range(H):
        for q in range(C):
            greet(H * c + h, jnp.int32(q))
    pl.semaphore_wait(barrier, 3 * R - 1 - 2 * is_self.astype(jnp.int32))

    slot = lax.rem(r, H) * C + c

    def first_copy(t):
        return pltpu.make_async_remote_copy(
            src_ref=start, dst_ref=landed.at[slot], send_sem=first_send.at[t],
            recv_sem=first_recv.at[slot], device_id=(jnp.int32(t), home), device_id_type=MESH,
        )

    def not_self(t):
        return jnp.logical_not((r == t) & is_self)

    for t in range(R):
        @pl.when(not_self(t))
        def _():
            first_copy(t).start()

    @pl.when(is_self)
    def _():
        pltpu.make_async_copy(start, landed.at[slot], first_recv.at[slot]).start()

    row_id = lax.broadcasted_iota(jnp.int32, (rows, dirs.shape[2]), 0)
    wave_id = lax.broadcasted_iota(jnp.int32, (rows, dirs.shape[2]), 1)
    wave = c * (H * wl) + (row_id // (2 * wl)) * wl + row_id % wl
    chosen = wave_id == wave
    for a in range(halves):
        column = [
            jnp.sum(jnp.where(chosen, dirs[a, k : k + 1, :], 0.0), axis=1, keepdims=True)
            for k in range(3)
        ]
        for i in range(quad.shape[0]):
            lanes = pl.ds(i * 128, 128)
            q = quad[i : i + 1, :]
            weights[a, :, lanes] = (
                column[0] * (coords[0:1, lanes] * q)
                + column[1] * (coords[1:2, lanes] * q)
                + column[2] * (coords[2:3, lanes] * q)
            )

    O = modes.shape[0]
    chip = lax.rem(r, 8) // 2
    near = r // 8 * 4 + (jnp.clip(chip, 1, 2) - 1) * 2 + lax.rem(r, 2)
    owner = (chip == 1) | (chip == 2)

    def block(o):
        return pl.ds(pl.multiple_of(o * own, own), own)

    part_id = (lax.broadcasted_iota(jnp.int32, (rows, coords.shape[1]), 0) // wl) % 2

    def scale(total, a):
        v = total * weights[a]
        turned = jnp.where(part_id == 0, pltpu.roll(v, rows - wl, 0), -pltpu.roll(v, wl, 0))
        scaled[...] = turned.astype(jnp.bfloat16)

    basis_copy.wait()
    width = start.shape[2]
    total = jnp.zeros((rows, coords.shape[1]), jnp.float32)
    for q in range(C):
        lanes = pl.ds(q * width, width)
        for h in range(H):
            pltpu.make_async_copy(start, landed.at[h * C + q], first_recv.at[h * C + q]).wait()
            for x in range(2):
                joined[pl.ds((h * 2 + x) * wl, wl), lanes] = landed[h * C + q, x].astype(
                    jnp.float32
                )
        total = total + lax.dot_general(
            joined[:, lanes].astype(jnp.bfloat16), basis[:, lanes], NT,
            preferred_element_type=jnp.float32,
        )
    scale(total, 0)

    @pl.when(owner)
    def _():
        piece = joined[:, block(near)]
        field[...] = piece
        modes[near] = piece.astype(jnp.bfloat16)

    def sum_copy(j):
        o = near ^ j
        return pltpu.make_async_remote_copy(
            src_ref=parts.at[j], dst_ref=sums.at[r], send_sem=sum_send.at[j],
            recv_sem=sum_recv.at[r], device_id=(o // 4 * 8 + 2 + lax.rem(o, 4), c),
            device_id_type=MESH,
        )

    def mode_copy(d):
        return pltpu.make_async_remote_copy(
            src_ref=modes.at[near], dst_ref=modes.at[near], send_sem=mode_send.at[d],
            recv_sem=mode_recv.at[near], device_id=(r ^ d, c), device_id_type=MESH,
        )

    def send_parts():
        v = scaled[...]
        for j in reversed(range(O)):
            part = lax.dot_general(
                v, basis[:, block(near ^ j)], NN, preferred_element_type=jnp.float32
            )
            if j > 0:
                parts[j] = part.astype(jnp.bfloat16)
                sum_copy(j).start()
            else:
                acc[...] = part
        @pl.when(jnp.logical_not(owner))
        def _():
            parts[0] = acc[...].astype(jnp.bfloat16)
            sum_copy(0).start()

    def wait_parts():
        for j in range(1, O):
            sum_copy(j).wait_send()

        @pl.when(jnp.logical_not(owner))
        def _():
            sum_copy(0).wait_send()

    def own_block(factor, keep):
        result = acc[...]
        for d in range(1, R):
            t = r ^ d
            pltpu.make_async_copy(parts.at[0], sums.at[t], sum_recv.at[t]).wait()
            result = result + sums[t].astype(jnp.float32)
        lam = jnp.concatenate(
            [rates[pl.ds(near * (own // 128) + i, 1), :] for i in range(own // 128)], axis=1
        )
        return factor * result + (keep - factor * lam) * modes[near].astype(jnp.float32)

    def half_step(i, carry):
        odd = lax.rem(i, 2) == 1
        factor = jnp.where(odd, 1.0, 0.5).astype(jnp.float32)
        keep = jnp.where(odd, 0.0, 1.0).astype(jnp.float32)
        send_parts()

        @pl.when(owner)
        def _():
            fresh = own_block(factor, keep) + (1.0 - keep) * field[...]
            rounded = fresh.astype(jnp.bfloat16)
            modes[near] = rounded
            for d in reversed(range(1, R)):
                mode_copy(d).start()

            @pl.when(odd)
            def _():
                field[...] = rounded.astype(jnp.float32)

        total = jnp.zeros((rows, coords.shape[1]), jnp.float32)
        for j in range(O):
            o = near ^ j

            def arrive():
                pltpu.make_async_copy(parts.at[0], modes.at[o], mode_recv.at[o]).wait()

            if j == 0:
                pl.when(jnp.logical_not(owner))(arrive)
            else:
                arrive()
            total = total + lax.dot_general(
                modes[o], basis[:, block(o)], NT, preferred_element_type=jnp.float32
            )
        scale(total, i + 1)
        wait_parts()

        @pl.when(owner)
        def _():
            for d in range(1, R):
                mode_copy(d).wait_send()
        return carry

    lax.fori_loop(0, halves - 1, half_step, 0)

    send_parts()
    F = O // C
    target_col = near // F
    slot_out = lax.rem(near, F)

    def last_copy(h):
        return pltpu.make_async_remote_copy(
            src_ref=lastout.at[h], dst_ref=lastin.at[slot_out], send_sem=last_send.at[h],
            recv_sem=last_recv.at[slot_out], device_id=(H * c + h, target_col),
            device_id_type=MESH,
        )

    def local(h):
        return (H * c + h == r) & (target_col == c)

    @pl.when(owner)
    def _():
        fresh = own_block(1.0, 0.0) + field[...]
        for h in range(H):
            for x in range(2):
                first = (h * 2 + x) * wl
                lastout[h, x] = fresh[first : first + wl, :].astype(jnp.bfloat16)

            @pl.when(jnp.logical_not(local(h)))
            def _():
                last_copy(h).start()

            @pl.when(local(h))
            def _():
                pltpu.make_async_copy(
                    lastout.at[h], lastin.at[slot_out], last_recv.at[slot_out]
                ).start()

    for s in range(F):
        pltpu.make_async_copy(lastout.at[0], lastin.at[s], last_recv.at[s]).wait()
        out[:, :, pl.ds(s * own, own)] = lastin[s]

    @pl.when(owner)
    def _():
        for h in range(H):
            @pl.when(jnp.logical_not(local(h)))
            def _():
                last_copy(h).wait_send()

    wait_parts()
    for t in range(R):
        @pl.when(not_self(t))
        def _():
            first_copy(t).wait_send()


def on_device(R, C, basis, coords, quad, magnetization, rates, dirs):
    H = R // C
    nodes, mode_count = basis.shape
    start = jnp.transpose(magnetization, (0, 2, 1))
    _, wl, width = start.shape
    rows = H * 2 * wl
    O = R // 2
    own = mode_count // O
    F = O // C
    vmem = pl.BlockSpec(memory_space=pltpu.VMEM)
    dma = pltpu.SemaphoreType.DMA
    bf16, f32 = jnp.bfloat16, jnp.float32
    result = pl.pallas_call(
        functools.partial(kernel, R, C),
        out_shape=jax.ShapeDtypeStruct(start.shape, bf16),
        in_specs=[pl.BlockSpec(memory_space=pl.ANY)] + [vmem] * 5,
        out_specs=vmem,
        scratch_shapes=[
            pltpu.VMEM((nodes, mode_count), bf16),
            pltpu.VMEM((H * C, 2, wl, width), bf16),
            pltpu.VMEM((rows, mode_count), f32),
            pltpu.VMEM((O, rows, own), bf16),
            pltpu.VMEM((O, rows, own), bf16),
            pltpu.VMEM((R, rows, own), bf16),
            pltpu.VMEM((2 * STEPS, rows, nodes), f32),
            pltpu.VMEM((rows, nodes), bf16),
            pltpu.VMEM((rows, own), f32),
            pltpu.VMEM((rows, own), f32),
            pltpu.VMEM((H, 2, wl, own), bf16),
            pltpu.VMEM((F, 2, wl, own), bf16),
            dma,
            dma((R,)), dma((H * C,)),
            dma((O,)), dma((R,)), dma((R,)), dma((O,)),
            dma((H,)), dma((F,)),
        ],
        compiler_params=pltpu.CompilerParams(collective_id=0, has_side_effects=True),
    )(basis, coords, quad.reshape(-1, 128), start, rates.reshape(-1, 128), dirs)
    return jnp.transpose(result, (0, 2, 1))


def solution(mesh):
    return jax.shard_map(
        functools.partial(on_device, mesh.shape["row"], mesh.shape["col"]),
        mesh=mesh,
        in_specs=(P("row", None), P(None, "row"), P("row"), P(None, "col", "row"), P(), P()),
        out_specs=P(None, "col", "row"),
        check_vma=False,
    )
```

```python
import functools

import jax
import jax.numpy as jnp
from jax import lax
from jax.experimental import pallas as pl
from jax.experimental.pallas import tpu as pltpu
from jax.sharding import PartitionSpec as P

STEPS = 3
MESH = pl.DeviceIdType.MESH
NT = (((1,), (1,)), ((), ()))
NN = (((1,), (0,)), ((), ()))


def kernel(
    R, C, basis_hbm, coords, quad, start, rates, dirs, out,
    basis, landed, joined, modes, parts, sums, weights, scaled, field, lastout, lastin,
    basis_sem, first_send, first_recv, sum_send, sum_recv, mode_send, mode_recv,
    last_send, last_recv,
):
    H = R // C
    r = lax.axis_index("row")
    c = lax.axis_index("col")
    wl = start.shape[1]
    rows = H * 2 * wl
    own = modes.shape[2]
    halves = 2 * STEPS

    basis_copy = pltpu.make_async_copy(basis_hbm, basis, basis_sem)
    basis_copy.start()

    barrier = pltpu.get_barrier_semaphore()
    home = r // H
    for d in range(1, R):
        pl.semaphore_signal(barrier, inc=1, device_id=((r ^ d), c), device_id_type=MESH)
    is_self = home == c

    def greet(row, col):
        @pl.when(jnp.logical_not((row == r) & (col == c)))
        def _():
            pl.semaphore_signal(barrier, inc=1, device_id=(row, col), device_id_type=MESH)

    for t in range(R):
        greet(jnp.int32(t), home)
    for h in range(H):
        for q in range(C):
            greet(H * c + h, jnp.int32(q))
    pl.semaphore_wait(barrier, 3 * R - 1 - 2 * is_self.astype(jnp.int32))

    slot = lax.rem(r, H) * C + c

    def first_copy(t):
        return pltpu.make_async_remote_copy(
            src_ref=start, dst_ref=landed.at[slot], send_sem=first_send.at[t],
            recv_sem=first_recv.at[slot], device_id=(jnp.int32(t), home), device_id_type=MESH,
        )

    def not_self(t):
        return jnp.logical_not((r == t) & is_self)

    for t in range(R):
        @pl.when(not_self(t))
        def _():
            first_copy(t).start()

    @pl.when(is_self)
    def _():
        pltpu.make_async_copy(start, landed.at[slot], first_recv.at[slot]).start()

    row_id = lax.broadcasted_iota(jnp.int32, (rows, dirs.shape[2]), 0)
    wave_id = lax.broadcasted_iota(jnp.int32, (rows, dirs.shape[2]), 1)
    wave = c * (H * wl) + (row_id // (2 * wl)) * wl + row_id % wl
    chosen = wave_id == wave
    for a in range(halves):
        column = [
            jnp.sum(jnp.where(chosen, dirs[a, k : k + 1, :], 0.0), axis=1, keepdims=True)
            for k in range(3)
        ]
        for i in range(quad.shape[0]):
            lanes = pl.ds(i * 128, 128)
            q = quad[i : i + 1, :]
            weights[a, :, lanes] = (
                column[0] * (coords[0:1, lanes] * q)
                + column[1] * (coords[1:2, lanes] * q)
                + column[2] * (coords[2:3, lanes] * q)
            )

    width = start.shape[2]
    for h in range(H):
        for q in range(C):
            pltpu.make_async_copy(start, landed.at[h * C + q], first_recv.at[h * C + q]).wait()
            for x in range(2):
                joined[pl.ds((h * 2 + x) * wl, wl), pl.ds(q * width, width)] = landed[
                    h * C + q, x
                ].astype(jnp.float32)
    basis_copy.wait()

    near = list(range(R))

    def block(t):
        return pl.ds(pl.multiple_of(t * own, own), own)

    part_id = (lax.broadcasted_iota(jnp.int32, (rows, coords.shape[1]), 0) // wl) % 2

    def scale(total, a):
        v = total * weights[a]
        turned = jnp.where(part_id == 0, pltpu.roll(v, rows - wl, 0), -pltpu.roll(v, wl, 0))
        scaled[...] = turned.astype(jnp.bfloat16)

    total = jnp.zeros((rows, coords.shape[1]), jnp.float32)
    for d in near:
        t = (r ^ d)
        piece = joined[:, block(t)]
        if d == 0:
            field[...] = piece
        piece = piece.astype(jnp.bfloat16)
        if d == 0:
            modes[0] = piece
        total = total + lax.dot_general(
            piece, basis[:, block(t)], NT, preferred_element_type=jnp.float32
        )
    scale(total, 0)

    def sum_copy(d):
        return pltpu.make_async_remote_copy(
            src_ref=parts.at[d], dst_ref=sums.at[d], send_sem=sum_send.at[d],
            recv_sem=sum_recv.at[d], device_id=((r ^ d), c), device_id_type=MESH,
        )

    def mode_copy(d):
        return pltpu.make_async_remote_copy(
            src_ref=modes.at[0], dst_ref=modes.at[d], send_sem=mode_send.at[d],
            recv_sem=mode_recv.at[d], device_id=((r ^ d), c), device_id_type=MESH,
        )

    def own_block(factor, keep):
        v = scaled[...]
        for d in reversed(near[1:]):
            t = (r ^ d)
            parts[d] = lax.dot_general(
                v, basis[:, block(t)], NN, preferred_element_type=jnp.float32
            ).astype(jnp.bfloat16)
            sum_copy(d).start()
        acc = lax.dot_general(v, basis[:, block(r)], NN, preferred_element_type=jnp.float32)
        for d in near[1:]:
            sum_copy(d).wait_recv()
            acc = acc + sums[d].astype(jnp.float32)
        lam = jnp.concatenate(
            [rates[pl.ds(r * (own // 128) + i, 1), :] for i in range(own // 128)], axis=1
        )
        return factor * acc + (keep - factor * lam) * modes[0].astype(jnp.float32)

    def half_step(i, carry):
        odd = lax.rem(i, 2) == 1
        factor = jnp.where(odd, 1.0, 0.5).astype(jnp.float32)
        keep = jnp.where(odd, 0.0, 1.0).astype(jnp.float32)
        fresh = own_block(factor, keep)
        fresh = fresh + (1.0 - keep) * field[...]
        rounded = fresh.astype(jnp.bfloat16)
        modes[0] = rounded
        for d in reversed(near[1:]):
            mode_copy(d).start()

        @pl.when(odd)
        def _():
            field[...] = rounded.astype(jnp.float32)

        total = lax.dot_general(
            rounded, basis[:, block(r)], NT, preferred_element_type=jnp.float32
        )
        for d in near[1:]:
            mode_copy(d).wait_recv()
            total = total + lax.dot_general(
                modes[d], basis[:, block((r ^ d))], NT,
                preferred_element_type=jnp.float32,
            )
        scale(total, i + 1)
        for d in near[1:]:
            sum_copy(d).wait_send()
        for d in near[1:]:
            mode_copy(d).wait_send()
        return carry

    lax.fori_loop(0, halves - 1, half_step, 0)

    fresh = own_block(1.0, 0.0) + field[...]
    target_col = r // H
    q = lax.rem(r, H)

    def last_copy(h):
        return pltpu.make_async_remote_copy(
            src_ref=lastout.at[h], dst_ref=lastin.at[q], send_sem=last_send.at[h],
            recv_sem=last_recv.at[q], device_id=(H * c + h, target_col), device_id_type=MESH,
        )

    for h in range(H):
        for x in range(2):
            first = (h * 2 + x) * wl
            lastout[h, x] = fresh[first : first + wl, :].astype(jnp.bfloat16)
        local = (H * c + h == r) & (target_col == c)

        @pl.when(jnp.logical_not(local))
        def _():
            last_copy(h).start()

        @pl.when(local)
        def _():
            pltpu.make_async_copy(lastout.at[h], lastin.at[q], last_recv.at[q]).start()

    for s in range(H):
        pltpu.make_async_copy(lastout.at[0], lastin.at[s], last_recv.at[s]).wait()
        out[:, :, pl.ds(s * own, own)] = lastin[s]
    for d in near[1:]:
        sum_copy(d).wait_send()
    for h in range(H):
        @pl.when(jnp.logical_not((H * c + h == r) & (target_col == c)))
        def _():
            last_copy(h).wait_send()
    for t in range(R):
        @pl.when(not_self(t))
        def _():
            first_copy(t).wait_send()


def on_device(R, C, basis, coords, quad, magnetization, rates, dirs):
    H = R // C
    nodes, mode_count = basis.shape
    start = jnp.transpose(magnetization, (0, 2, 1))
    _, wl, width = start.shape
    rows = H * 2 * wl
    own = mode_count // R
    vmem = pl.BlockSpec(memory_space=pltpu.VMEM)
    dma = pltpu.SemaphoreType.DMA
    bf16, f32 = jnp.bfloat16, jnp.float32
    result = pl.pallas_call(
        functools.partial(kernel, R, C),
        out_shape=jax.ShapeDtypeStruct(start.shape, bf16),
        in_specs=[pl.BlockSpec(memory_space=pl.ANY)] + [vmem] * 5,
        out_specs=vmem,
        scratch_shapes=[
            pltpu.VMEM((nodes, mode_count), bf16),
            pltpu.VMEM((H * C, 2, wl, width), bf16),
            pltpu.VMEM((rows, mode_count), f32),
            pltpu.VMEM((R, rows, own), bf16),
            pltpu.VMEM((R, rows, own), bf16),
            pltpu.VMEM((R, rows, own), bf16),
            pltpu.VMEM((2 * STEPS, rows, nodes), f32),
            pltpu.VMEM((rows, nodes), bf16),
            pltpu.VMEM((rows, own), f32),
            pltpu.VMEM((H, 2, wl, own), bf16),
            pltpu.VMEM((H, 2, wl, own), bf16),
            dma,
            dma((R,)), dma((H * C,)),
            dma((R,)), dma((R,)), dma((R,)), dma((R,)),
            dma((H,)), dma((H,)),
        ],
        compiler_params=pltpu.CompilerParams(collective_id=0, has_side_effects=True),
    )(basis, coords, quad.reshape(-1, 128), start, rates.reshape(-1, 128), dirs)
    return jnp.transpose(result, (0, 2, 1))


def solution(mesh):
    return jax.shard_map(
        functools.partial(on_device, mesh.shape["row"], mesh.shape["col"]),
        mesh=mesh,
        in_specs=(P("row", None), P(None, "row"), P("row"), P(None, "col", "row"), P(), P()),
        out_specs=P(None, "col", "row"),
        check_vma=False,
    )
```
